32 devices in a mesh: gx: 8 (over z, core), gy: 4 (over y, x).
Axes of the slice: x: 2, y: 2, z: 4, core: 2. Of those that a mesh axis runs over, the one named last changes fastest.
Arguments:
- hidden_in: bfloat16 [1024, 8192], P('gy', 'gx'), may hold values from -1200 to 1200
- norm_gain: bfloat16 [8192], P('gx'), may hold values from 0.099609375 to 1.8984375
- wq: bfloat16 [8192, 8192], P('gx', 'gy'), may hold values from -0.0625 to 0.0625
- wkv: bfloat16 [8192, 2, 1024], P('gx', None, 'gy'), may hold values from -0.125 to 0.125
- wo: bfloat16 [8192, 8192], P('gy', 'gx'), may hold values from -0.5 to 0.5
- kv_cache: bfloat16 [2, 8192, 1024], P(None, 'gx', 'gy'), may hold values from -200 to 200
- start: int32 [1], replicated, may hold values from 2048 to 8192
Outputs:
- attn_out: bfloat16 [1024, 8192], P('gy', 'gx')
The draws below stay inside these ranges and needn't reach their ends.
All inputs are finite; a program needn't handle non-finite values.
Results may differ from the reference program's by a relative error of at most 0.009.
The reference program's roundings to bfloat16 on the way count: a program that leaves them out, or rounds other values in their place, can miss the bound.
Values may be sent and summed in bfloat16 or wider, within the bound.
A program may use at most 320 MiB of HBM per device.

```python
import jax
import jax.numpy as jnp
from jax import lax

D = 8192
HQ = 64
KVH = 8
HD = 128
TOKENS = 1024
CACHE = 8192


def draw_hidden_in(key, part):
    sub_keys = jax.random.split(key, 3)
    row_scale = 10.0 ** jax.random.uniform(sub_keys[1], (TOKENS, 1), jnp.float32)
    rising = 3.0 ** (jnp.arange(D, dtype=jnp.float32) / (D - 1))
    column_scale = 10.0 ** jax.random.uniform(sub_keys[2], (1, D), jnp.float32) * rising[None, :]
    entries = jax.random.truncated_normal(sub_keys[0], -4.0, 4.0, (TOKENS, D), jnp.float32)
    return (entries * row_scale * column_scale).astype(jnp.bfloat16)


def draw_kv_cache(key, part):
    sub_keys = jax.random.split(key, 1)
    shape = (2, CACHE, KVH * HD)
    entries = 2.0 * jax.random.truncated_normal(sub_keys[0], -5.0, 5.0, shape, jnp.float32)
    return entries.astype(jnp.bfloat16)


def steps_of(key, shape, shards, low, top_value):
    loudness = 1.0
    for dim, blocks in shards:
        heights = jax.random.uniform(jax.random.fold_in(jax.random.fold_in(key, 6), dim), (blocks,), jnp.float32, low / len(shards), top_value / len(shards))
        loudness = loudness * jnp.repeat(jnp.exp(heights), shape[dim] // blocks).reshape((-1,) + (1,) * (len(shape) - 1 - dim))
    return loudness


def scatter_about(stream_key, dims, scale, bound, cuts=(), kind=jnp.bfloat16):
    result = scale * jax.random.normal(stream_key, dims, jnp.float32)
    if cuts:
        result = result * steps_of(stream_key, dims, cuts, -0.22, 0.18)
    return jnp.clip(result, -bound, bound).astype(kind)


def setup_inputs(seed: int = 0) -> dict:
    key_list = jax.random.split(jax.random.key(seed), 8)
    hidden_in = draw_hidden_in(jax.random.fold_in(key_list[7], 71), 0)
    norm_gain = jnp.clip(1.0 + 0.18 * jax.random.normal(key_list[1], (D,), jnp.float32), 0.099609375, 1.8984375).astype(jnp.bfloat16)
    wq = scatter_about(key_list[2], (D, HQ * HD), D ** -0.5, 0.0625, ((0, 8), (1, 4)))
    wkv = scatter_about(key_list[3], (D, 2, KVH * HD), (D // 4) ** -0.5, 0.125, ((0, 8), (2, 4)))
    wo = scatter_about(key_list[4], (HQ * HD, D), HD ** -0.5, 0.5, ((0, 4), (1, 8)))
    kv_cache = draw_kv_cache(jax.random.fold_in(key_list[7], 71), 0)
    start = jax.random.randint(key_list[6], (1,), CACHE // 4, CACHE + 1).astype(jnp.int32)
    return dict(hidden_in=hidden_in, norm_gain=norm_gain, wq=wq, wkv=wkv, wo=wo, kv_cache=kv_cache, start=start)


NEG_FILL = -1e+30

def reference(hidden_in, norm_gain, wq, wkv, wo, kv_cache, start):
    as_float = hidden_in.astype(jnp.float32)
    mean_square = lax.optimization_barrier(jnp.mean(as_float * as_float, axis=1, keepdims=True))
    normed = (as_float * lax.rsqrt(mean_square + 1e-05) * norm_gain.astype(jnp.float32)[None, :]).astype(jnp.bfloat16)
    queries = jnp.dot(normed, wq, preferred_element_type=jnp.float32).astype(jnp.bfloat16)
    fresh = jnp.dot(normed, wkv.reshape(D, 2 * KVH * HD), preferred_element_type=jnp.float32).astype(jnp.bfloat16)
    fresh = fresh.reshape(TOKENS, 2, KVH * HD)
    key_rows = jnp.concatenate([kv_cache[0], fresh[:, 0]], axis=0)
    value_rows = jnp.concatenate([kv_cache[1], fresh[:, 1]], axis=0)
    anchor = start[0]
    key_index = jnp.arange(CACHE + TOKENS, dtype=jnp.int32)
    query_index = jnp.arange(TOKENS, dtype=jnp.int32)
    visible = jnp.where((key_index < CACHE)[None, :], (key_index < anchor)[None, :], (key_index - CACHE)[None, :] <= query_index[:, None])
    per_group = HQ // KVH
    score_scale = HD ** (-0.5)

    def one_head(head_index):
        group_index = head_index // per_group
        query_head = lax.dynamic_slice_in_dim(queries, head_index * HD, HD, 1).astype(jnp.float32)
        key_head = lax.dynamic_slice_in_dim(key_rows, group_index * HD, HD, 1).astype(jnp.float32)
        value_head = lax.dynamic_slice_in_dim(value_rows, group_index * HD, HD, 1).astype(jnp.float32)
        scores = jnp.dot(query_head, key_head.T, precision=lax.Precision.HIGHEST) * score_scale
        scores = jnp.where(visible, scores, NEG_FILL)
        row_peak = lax.optimization_barrier(jnp.max(scores, axis=1, keepdims=True))
        weights = jnp.where(visible, jnp.exp(scores - row_peak), 0.0)
        totals = lax.optimization_barrier(jnp.sum(weights, axis=1, keepdims=True))
        probs = lax.optimization_barrier(weights.astype(jnp.bfloat16))
        summed = jnp.dot(probs.astype(jnp.float32), value_head, precision=lax.Precision.HIGHEST)
        return (summed / totals).astype(jnp.bfloat16)
    heads = lax.map(one_head, jnp.arange(HQ, dtype=jnp.int32))
    heads = jnp.transpose(heads, (1, 0, 2)).reshape(TOKENS, HQ * HD)
    return jnp.dot(heads, wo, preferred_element_type=jnp.float32).astype(jnp.bfloat16)
```

```python
import functools
import math

import jax
import jax.numpy as jnp
from jax import lax
from jax.experimental import pallas as pl
from jax.experimental.pallas import tpu as pltpu
from jax.sharding import PartitionSpec as P

HD = 128
NEG_FILL = -1e30
EPSILON = 1e-05
LOG2E = 1.4426950408889634


def attention_kernel(heads_per_step, regions, info_ref, q_ref, *refs):
    caches = refs[:regions]
    fresh_ref, out_ref = refs[regions:]
    rows = q_ref.shape[0]
    pieces, _, length, _ = caches[0].shape
    scale = (HD ** -0.5) * LOG2E
    queries = [q_ref[:, h * HD : (h + 1) * HD] for h in range(heads_per_step)]

    def step(carried, keys, values, mask):
        result = []
        scores = [
            lax.dot_general(q, keys, (((1,), (1,)), ((), ())), preferred_element_type=jnp.float32)
            for q in queries
        ]
        for (peak, totals, summed), score in zip(carried, scores):
            if mask is not None:
                score = jnp.where(mask, score, NEG_FILL)
            higher = jnp.maximum(peak, jnp.max(score, axis=1, keepdims=True))
            weights = jnp.exp2((score - higher) * scale)
            factor = jnp.exp2((peak - higher) * scale)
            totals = totals * factor + jnp.sum(weights, axis=1, keepdims=True)
            summed = summed * factor + jnp.dot(
                weights.astype(jnp.bfloat16), values, preferred_element_type=jnp.float32
            )
            result.append((higher, totals, summed))
        return tuple(result)

    carried = tuple(
        (
            jnp.full((rows, 1), NEG_FILL, jnp.float32),
            jnp.zeros((rows, 1), jnp.float32),
            jnp.zeros((rows, HD), jnp.float32),
        )
        for _ in range(heads_per_step)
    )
    for region, cache in enumerate(caches):
        live = info_ref[region]
        full = live // length
        carried = lax.fori_loop(
            0, full, lambda j, c, cache=cache: step(c, cache[j, 0], cache[j, 1], None), carried
        )
        rest = live - full * length

        def tail(c, cache=cache, full=full, rest=rest):
            mask = lax.broadcasted_iota(jnp.int32, (rows, length), 1) < rest
            return step(c, cache[full, 0], cache[full, 1], mask)

        carried = lax.cond(rest > 0, tail, lambda c: c, carried)
    own = info_ref[regions]
    carried = lax.fori_loop(
        0, own, lambda j, c: step(c, fresh_ref[j, :, :HD], fresh_ref[j, :, HD:], None), carried
    )
    causal = lax.broadcasted_iota(jnp.int32, (rows, rows), 1) <= lax.broadcasted_iota(
        jnp.int32, (rows, rows), 0
    )
    carried = step(carried, fresh_ref[own, :, :HD], fresh_ref[own, :, HD:], causal)
    for h, (_, totals, summed) in enumerate(carried):
        out_ref[:, h * HD : (h + 1) * HD] = (summed / totals).astype(jnp.bfloat16)


def attention(info, queries, caches, fresh, heads_per_step=2):
    rows, cols = queries.shape
    heads = cols // HD
    width = heads_per_step * HD
    whole = lambda a: pl.BlockSpec(a.shape, lambda i, s, n=a.ndim: (0,) * n)
    return pl.pallas_call(
        functools.partial(attention_kernel, heads_per_step, len(caches)),
        out_shape=jax.ShapeDtypeStruct((rows, cols), jnp.bfloat16),
        grid_spec=pltpu.PrefetchScalarGridSpec(
            num_scalar_prefetch=1,
            grid=(heads // heads_per_step,),
            in_specs=[pl.BlockSpec((rows, width), lambda i, s: (0, i))]
            + [whole(c) for c in caches]
            + [whole(fresh)],
            out_specs=pl.BlockSpec((rows, width), lambda i, s: (0, i)),
        ),
        compiler_params=pltpu.CompilerParams(vmem_limit_bytes=50 * 1024 * 1024),
    )(info, queries, *caches, fresh)


def local(hidden_in, norm_gain, wq, wkv, wo, kv_cache, start):
    devices_x = lax.axis_size("gx")
    width_all = hidden_in.shape[1] * devices_x
    position = lax.axis_index("gx")
    groups = wkv.shape[2] // HD
    query_cols = wq.shape[1] // groups
    members = devices_x // groups
    part = position // members
    member = position % members
    teams = [[g * members + i for i in range(members)] for g in range(groups)]

    slots = kv_cache.shape[1]
    pieces = jnp.stack([kv_cache[:, :, g * HD : (g + 1) * HD] for g in range(groups)])
    caches = []
    live = []
    for shift in range(groups):
        source = (part + shift) % groups
        piece = pieces[(part - shift) % groups] if groups > 1 else pieces[0]
        if shift:
            pairs = [
                (j, ((j // members - shift) % groups) * members + j % members)
                for j in range(devices_x)
            ]
            piece = lax.ppermute(piece, "gx", pairs)
        caches.append(lax.all_gather(piece, "gx", axis=0, axis_index_groups=teams))
        span = members * slots
        live.append(jnp.clip(start[0] - source * span, 0, span))
    info = jnp.stack(live + [member]).astype(jnp.int32)

    own_rows = hidden_in.astype(jnp.float32)
    squares = lax.all_gather(jnp.sum(own_rows * own_rows, axis=1), ("gx", "gy"), axis=0)
    hidden = lax.all_gather(hidden_in, "gy", axis=0, tiled=True)
    tokens = hidden.shape[0]
    squares = jnp.sum(squares.reshape(devices_x, tokens), axis=0)
    normed = (
        hidden.astype(jnp.float32)
        * lax.rsqrt(squares / width_all + EPSILON)[:, None]
        * norm_gain.astype(jnp.float32)[None, :]
    ).astype(jnp.bfloat16)

    def project(weights):
        return jnp.dot(normed, weights, preferred_element_type=jnp.float32)

    width_in = wkv.shape[0]
    fresh = jnp.concatenate(
        [
            project(wkv[:, :, g * HD : (g + 1) * HD].reshape(width_in, 2 * HD))
            for g in range(groups)
        ]
    )
    fresh = lax.psum_scatter(fresh, "gx", scatter_dimension=0, tiled=True).astype(jnp.bfloat16)
    fresh = lax.all_gather(fresh, "gx", axis=0, axis_index_groups=teams)
    queries = jnp.concatenate(
        [project(wq[:, g * query_cols : (g + 1) * query_cols]) for g in range(groups)]
    )
    queries = lax.psum_scatter(queries, "gx", scatter_dimension=0, tiled=True).astype(jnp.bfloat16)

    heads = attention(info, queries, caches, fresh)

    heads = lax.all_gather(heads, "gx", axis=0, tiled=True).reshape(groups, tokens, query_cols)
    result = jnp.dot(heads[0], wo[:query_cols], preferred_element_type=jnp.float32)
    for g in range(1, groups):
        result += jnp.dot(
            heads[g],
            wo[g * query_cols : (g + 1) * query_cols],
            preferred_element_type=jnp.float32,
        )
    return lax.psum_scatter(
        result.astype(jnp.bfloat16), "gy", scatter_dimension=0, tiled=True
    )


def solution(mesh):
    in_specs = (
        P("gy", "gx"),
        P("gx"),
        P("gx", "gy"),
        P("gx", None, "gy"),
        P("gy", "gx"),
        P(None, "gx", "gy"),
        P(),
    )
    out_specs = P("gy", "gx")
    return jax.shard_map(local, mesh=mesh, in_specs=in_specs, out_specs=out_specs, check_vma=False)
```
